32 devices in a mesh: row: 8 (over z, x), col: 4 (over y, core).
Axes of the slice: x: 2, y: 2, z: 4, core: 2. Of those that a mesh axis runs over, the one named last changes fastest.
Arguments:
- c_matrix: float32 [3072, 3072], P('row', 'col'), may hold values from -6 to 6
- a_upper: bfloat16 [3072, 3072], P('row', 'col'), may hold values from -0.3125 to 0.3125
- b_upper: bfloat16 [3072, 3072], P('row', 'col'), may hold values from -0.3125 to 0.3125
- a_vectors: bfloat16 [3072, 384], P('row'), may hold values from -1 to 2, as said below
- a_inverse: bfloat16 [3072, 384], P('row'), may hold values from -1 to 2, as said below
- b_vectors: bfloat16 [3072, 384], P('row'), may hold values from -1 to 2, as said below
- b_inverse: bfloat16 [3072, 384], P('row'), may hold values from -1 to 2, as said below
- a_values: bfloat16 [3072], P('row'), may hold values from 0.5 to 4
- b_values: bfloat16 [3072], P('row'), may hold values from 0.5 to 4
Outputs:
- overwritten: float32 [3072, 3072], P('row', 'col')
The draws below stay inside these ranges and needn't reach their ends.
Inputs may be any that keep to these rules, and one draw needn't show every extreme that they name: `a_vectors`: each 384 x 384 tile is an identity matrix plus independent entries of deviation about 0.5 / sqrt(384). `a_inverse`: each 384 x 384 tile is an identity matrix plus independent entries of deviation about 0.5 / sqrt(384). `b_vectors`: each 384 x 384 tile is an identity matrix plus independent entries of deviation about 0.5 / sqrt(384). `b_inverse`: each 384 x 384 tile is an identity matrix plus independent entries of deviation about 0.5 / sqrt(384).
All inputs are finite; a program needn't handle non-finite values.
Results may differ from the reference program's by a relative error of at most 0.012.
Values may be sent and summed in bfloat16 or wider, within the bound.
A program may use at most 64 MiB of HBM per device.

```python
import math
import jax
import jax.numpy as jnp

TILE = 384
WAVES = 3
W = 3072


def eigen_tiles(key):
    blocks = W // TILE
    jitter = jnp.clip(jax.random.normal(key, (W, TILE), jnp.float32), -4.0, 4.0)
    identity = jnp.tile(jnp.eye(TILE, dtype=jnp.float32), (blocks, 1))
    return (identity + 0.5 * jitter / math.sqrt(TILE)).astype(jnp.bfloat16)


def draw_a_vectors(key, part):
    return eigen_tiles(jax.random.fold_in(key, 11))


def draw_a_inverse(key, part):
    return eigen_tiles(jax.random.fold_in(key, 23))


def draw_b_vectors(key, part):
    return eigen_tiles(jax.random.fold_in(key, 37))


def draw_b_inverse(key, part):
    return eigen_tiles(jax.random.fold_in(key, 41))


def steps_of(stream_key, dims, cuts, smallest, largest):
    def one(position, parts):
        draws = jax.random.uniform(jax.random.fold_in(jax.random.fold_in(stream_key, 6), position), (parts,), jnp.float32, smallest / len(cuts), largest / len(cuts))
        return jnp.repeat(jnp.exp(draws), dims[position] // parts).reshape((-1,) + (1,) * (len(dims) - position - 1))

    gain = one(*cuts[0])
    for cut in cuts[1:]:
        gain = gain * one(*cut)
    return gain


def centred(rng, extent, width, limit, cuts=(), kind=jnp.bfloat16):
    drawn = jax.random.normal(rng, extent, jnp.float32) * width
    if len(cuts) > 0:
        drawn = steps_of(rng, extent, cuts, -0.22, 0.18) * drawn
    return jnp.clip(drawn, min=-limit, max=limit).astype(kind)


def setup_inputs(seed: int = 0) -> dict:
    streams_of = jax.random.split(jax.random.key(seed), 10)
    c_matrix = centred(streams_of[0], (W, W), 1.0, 6.0, ((0, 8), (1, 4)), jnp.float32)
    a_upper = centred(streams_of[1], (W, W), TILE ** -0.5, 0.3125, ((0, 8), (1, 4)))
    b_upper = centred(streams_of[2], (W, W), TILE ** -0.5, 0.3125, ((0, 8), (1, 4)))
    a_vectors = draw_a_vectors(jax.random.fold_in(streams_of[9], 71), 0)
    a_inverse = draw_a_inverse(jax.random.fold_in(streams_of[9], 71), 0)
    b_vectors = draw_b_vectors(jax.random.fold_in(streams_of[9], 71), 0)
    b_inverse = draw_b_inverse(jax.random.fold_in(streams_of[9], 71), 0)
    a_values = jnp.clip(jnp.exp(math.log(4.0) - 2.0794415 * jax.random.uniform(streams_of[7], (W,), jnp.float32) ** steps_of(streams_of[7], (W,), ((0, 8),), -0.2, 0.2)), 0.5, 4.0).astype(jnp.bfloat16)
    b_values = jnp.clip(jnp.exp(math.log(4.0) - 2.0794415 * jax.random.uniform(streams_of[8], (W,), jnp.float32) ** steps_of(streams_of[8], (W,), ((0, 8),), -0.2, 0.2)), 0.5, 4.0).astype(jnp.bfloat16)
    return dict(c_matrix=c_matrix, a_upper=a_upper, b_upper=b_upper, a_vectors=a_vectors, a_inverse=a_inverse, b_vectors=b_vectors, b_inverse=b_inverse, a_values=a_values, b_values=b_values)


def batch_product(form, left, right):
    return jnp.einsum(form, left.astype(jnp.float32), right.astype(jnp.float32))


def reference(c_matrix, a_upper, b_upper, a_vectors, a_inverse, b_vectors, b_inverse, a_values, b_values):
    blocks = W // TILE
    state_tiles = c_matrix.reshape(blocks, TILE, blocks, TILE)
    left_vectors = a_vectors.reshape(blocks, TILE, TILE)
    left_inverse = a_inverse.reshape(blocks, TILE, TILE)
    right_vectors = b_vectors.reshape(blocks, TILE, TILE)
    right_inverse = b_inverse.reshape(blocks, TILE, TILE)
    left_values = a_values.reshape(blocks, TILE).astype(jnp.float32)
    right_values = b_values.reshape(blocks, TILE).astype(jnp.float32)
    tile_ids = jnp.arange(blocks).astype(jnp.int32)
    for offset in range(WAVES - 1, -1, -1):
        wave_count = blocks - offset
        col_index = jnp.arange(wave_count).astype(jnp.int32)
        row_index = col_index + offset
        residue = state_tiles[row_index, :, col_index, :]
        section_one = batch_product('jab,jbc->jac', left_inverse[row_index], residue.astype(jnp.bfloat16)).astype(jnp.bfloat16)
        second = batch_product('jab,jbc->jac', section_one, right_vectors[col_index])
        divisor = left_values[row_index][:, :, None] + right_values[col_index][:, None, :]
        scaled = (second / divisor).astype(jnp.bfloat16)
        section_three = batch_product('jab,jbc->jac', left_vectors[row_index], scaled).astype(jnp.bfloat16)
        solved = batch_product('jab,jbc->jac', section_three, right_inverse[col_index])
        state_tiles = state_tiles.at[row_index, :, col_index, :].set(solved)
        packed = solved.astype(jnp.bfloat16)
        a_columns = a_upper.reshape(W, blocks, TILE)[:, offset:, :]
        change = batch_product('kjt,jtu->jku', a_columns, packed).reshape(wave_count, blocks, TILE, TILE)
        keep_mask = tile_ids[None, :] < row_index[:, None]
        change = jnp.where(keep_mask[:, :, None, None], change, jnp.float32(0.0))
        state_tiles = state_tiles.at[:, :, :wave_count, :].add(-jnp.transpose(change, (1, 2, 0, 3)))
        b_strip = b_upper.reshape(blocks, TILE, W)[:wave_count]
        change = batch_product('jtu,juw->jtw', packed, b_strip).reshape(wave_count, TILE, blocks, TILE)
        keep_mask = tile_ids[None, :] > col_index[:, None]
        change = jnp.where(keep_mask[:, None, :, None], change, jnp.float32(0.0))
        state_tiles = state_tiles.at[offset:, :, :, :].add(-change)
    return state_tiles.reshape(W, W)
```

```python
import functools

import jax
import jax.numpy as jnp
from jax import lax
from jax.experimental import pallas as pl
from jax.experimental.pallas import tpu as pltpu
from jax.sharding import PartitionSpec as P

WAVES = 3
MEMBERS = 2
CHUNKS = 2
MESH = pl.DeviceIdType.MESH
f32 = jnp.float32
bf16 = jnp.bfloat16


def kernel(
    rows, cols, tile,
    c_hbm, a_hbm, b_hbm, u_hbm, p_hbm, v_hbm, q_hbm, lam_hbm, mu_hbm,
    out_hbm,
    state, abuf, bbuf, pbuf, ubuf, vbuf, qbuf, lam, mu, xr, xc,
    load_sem, out_sem,
    vq_send, vq_fsend, vq_recv,
    a_send, a_recv,
    b_send, b_fsend, b_recv,
    xr_send, xr_recv,
    xc_send, xc_recv,
):
    r = lax.axis_index("row")
    c = lax.axis_index("col")
    even_row = r % 2 == 0
    odd_row = r % 2 == 1
    even_col = c % 2 == 0
    step = tile // CHUNKS

    def dot(left, right):
        return jnp.dot(left, right, preferred_element_type=f32)

    def part(ref, member):
        return ref.at[:, pl.ds(member * tile, tile)]

    loads = []

    def load(source, target):
        copy = pltpu.make_async_copy(source, target, load_sem.at[len(loads)])
        copy.start()
        loads.append(copy)
        return copy

    ld_p = load(p_hbm, pbuf)
    ld_c = [load(part(c_hbm, m), state.at[m]) for m in range(MEMBERS)]
    ld_lam = load(lam_hbm, lam)
    ld_u = load(u_hbm, ubuf)
    ld_a = [load(part(a_hbm, m), abuf.at[m]) for m in range(MEMBERS)]
    ld_v = load(v_hbm, vbuf.at[0])
    ld_q = load(q_hbm, qbuf.at[0])
    ld_mu = load(mu_hbm, mu.at[0])
    ld_b = [load(part(b_hbm, m), bbuf.at[0, m]) for m in range(MEMBERS)]

    barrier = pltpu.get_barrier_semaphore()
    count = jnp.int32(0)
    for d in (-2, -1, 1, 2):
        there = (r + d >= 0) & (r + d < rows)
        count += there.astype(jnp.int32)

        @pl.when(there)
        def _():
            pl.semaphore_signal(barrier, inc=1, device_id=(r + d, c), device_id_type=MESH)

        there = (c + d >= 0) & (c + d < cols)
        count += there.astype(jnp.int32)

        @pl.when(there)
        def _():
            pl.semaphore_signal(barrier, inc=1, device_id=(r, c + d), device_id_type=MESH)

    pl.semaphore_wait(barrier, count)

    sends = []

    def remote(source, target, send, recv, to):
        return pltpu.make_async_remote_copy(
            src_ref=source, dst_ref=target, send_sem=send, recv_sem=recv,
            device_id=to, device_id_type=MESH,
        )

    def push(condition, *copy):
        @pl.when(condition)
        def _():
            remote(*copy).start()

        sends.append((condition, copy))

    def got(target, recv):
        remote(target, target, recv, recv, (r, c)).wait_recv()

    diagonal = c == r // MEMBERS
    sources = (v_hbm, q_hbm, mu_hbm)
    slots = (vbuf, qbuf, mu)
    for t in (2, 1):
        reach = diagonal & (r + t < rows)
        if t == 1:
            reach = reach & even_row
        for k in (0, 2, 1):
            push(reach, sources[k], slots[k].at[t], vq_send.at[t, k], vq_recv.at[t, k], (r + t, c))
    for m in range(MEMBERS):
        push(
            (c > 0) & (r < MEMBERS * c + m),
            part(a_hbm, m), abuf.at[MEMBERS + m], a_send.at[m], a_recv.at[m], (r, c - 1),
        )
    for t in (2, 1):
        for m in range(MEMBERS):
            reach = (MEMBERS * c + m > r) & (r + t < rows)
            if t == 1:
                reach = reach & even_row
            push(
                reach, part(b_hbm, m), bbuf.at[t, m], b_send.at[t, m], b_recv.at[t, m], (r + t, c)
            )

    def owns(s):
        j = r - s
        return (j >= 0) & (j // MEMBERS == c)

    def update(s, m, condition=None):
        j = MEMBERS * c + m
        i = j + s
        below = (i < rows) & (r < i)
        right = (r - s >= 0) & (j > r - s)
        if condition is not None:
            below = below & condition
            right = right & condition

        @pl.when(below)
        def _():
            state[m] = state[m] - dot(abuf[m + s], xc[s, m])

        @pl.when(right)
        def _():
            state[m] = state[m] - dot(xr[s], bbuf[s, m])

    for copy in (ld_p, *ld_c, ld_lam, ld_u):
        copy.wait()

    for s in range(WAVES - 1, -1, -1):
        mine = owns(s)
        m_own = jnp.clip(r - s - MEMBERS * c, 0, MEMBERS - 1)
        if s < WAVES - 1:
            update(s + 1, m_own, mine)
        if s == 0:
            ld_v.wait()
            ld_q.wait()
            ld_mu.wait()

        @pl.when(mine)
        def _():
            first = dot(pbuf[...], state[m_own].astype(bf16)).astype(bf16)
            if s > 0:
                got(vbuf.at[s], vq_recv.at[s, 0])
                got(mu.at[s], vq_recv.at[s, 2])
            second = dot(first, vbuf[s])
            scaled = (second / (lam[...] + mu[s])).astype(bf16)
            third = dot(ubuf[...], scaled).astype(bf16)
            if s > 0:
                got(qbuf.at[s], vq_recv.at[s, 1])
            solved = dot(third, qbuf[s])
            state[m_own] = solved
            xr[s] = solved.astype(bf16)

        for d in (1, 2):
            for h in range(CHUNKS):
                rng = pl.ds(h * step, step)
                push(
                    mine & (r - d >= 0),
                    xr.at[s, rng], xc.at[s, m_own, rng],
                    xc_send.at[s, MEMBERS + d - 1, h], xc_recv.at[s, m_own, h], (r - d, c),
                )
        held = (r - s >= 0) & (c >= (r - s) // MEMBERS)
        comes = (r - s >= 0) & (c > (r - s) // MEMBERS)
        for h in range(CHUNKS):
            rng = pl.ds(h * step, step)

            @pl.when(comes)
            def _():
                got(xr.at[s, rng], xr_recv.at[s, h])

            for d in (1, 2):
                reach = held & (c + d < cols)
                reach = reach & (even_col if d == 2 else (even_col | mine))
                push(
                    reach, xr.at[s, rng], xr.at[s, rng],
                    xr_send.at[s, d - 1, h], xr_recv.at[s, h], (r, c + d),
                )

        if s == WAVES - 1:
            for k in range(3):
                push(
                    mine & odd_row, slots[k].at[2], slots[k].at[1],
                    vq_fsend.at[k], vq_recv.at[1, k], (r - 1, c),
                )
        if s < WAVES - 1:
            for m in range(MEMBERS):
                update(s + 1, m, jnp.logical_not(mine & (m_own == m)))

        for h in range(CHUNKS):
            for m in range(MEMBERS):
                i = MEMBERS * c + m + s
                rng = pl.ds(h * step, step)
                comes = (i < rows) & (r < i)

                @pl.when(comes)
                def _():
                    got(xc.at[s, m, rng], xc_recv.at[s, m, h])

                push(
                    comes & (r - 2 >= 0), xc.at[s, m, rng], xc.at[s, m, rng],
                    xc_send.at[s, m, h], xc_recv.at[s, m, h], (r - 2, c),
                )

        if s == WAVES - 1:
            for copy in ld_a:
                copy.wait()
            for m in range(MEMBERS):
                @pl.when((c + 1 < cols) & (r < MEMBERS * (c + 1) + m))
                def _():
                    got(abuf.at[MEMBERS + m], a_recv.at[m])
        if s > 0:
            for m in range(MEMBERS):
                comes = (r - s >= 0) & (MEMBERS * c + m > r - s)

                @pl.when(comes)
                def _():
                    got(bbuf.at[s, m], b_recv.at[s, m])

                if s == WAVES - 1:
                    push(
                        comes & odd_row, bbuf.at[2, m], bbuf.at[1, m],
                        b_fsend.at[m], b_recv.at[1, m], (r - 1, c),
                    )
        else:
            for copy in ld_b:
                copy.wait()

    outs = []
    for m in range(MEMBERS):
        update(0, m)
        copy = pltpu.make_async_copy(state.at[m], part(out_hbm, m), out_sem.at[m])
        copy.start()
        outs.append(copy)
    for condition, copy in sends:
        @pl.when(condition)
        def _():
            remote(*copy).wait_send()
    for copy in outs:
        copy.wait()


def shards(
    c_matrix, a_upper, b_upper, a_vectors, a_inverse, b_vectors, b_inverse, a_values, b_values
):
    tile = a_vectors.shape[1]
    rows = lax.axis_size("row")
    cols = lax.axis_size("col")
    lam = a_values.astype(f32).reshape(tile, 1)
    mu = b_values.astype(f32).reshape(1, tile)
    dma = pltpu.SemaphoreType.DMA
    return pl.pallas_call(
        functools.partial(kernel, rows, cols, tile),
        out_shape=jax.ShapeDtypeStruct(c_matrix.shape, f32),
        in_specs=[pl.BlockSpec(memory_space=pl.ANY)] * 9,
        out_specs=pl.BlockSpec(memory_space=pl.ANY),
        scratch_shapes=[
            pltpu.VMEM((MEMBERS, tile, tile), f32),
            pltpu.VMEM((2 * MEMBERS, tile, tile), bf16),
            pltpu.VMEM((WAVES, MEMBERS, tile, tile), bf16),
            pltpu.VMEM((tile, tile), bf16),
            pltpu.VMEM((tile, tile), bf16),
            pltpu.VMEM((WAVES, tile, tile), bf16),
            pltpu.VMEM((WAVES, tile, tile), bf16),
            pltpu.VMEM((tile, 1), f32),
            pltpu.VMEM((WAVES, 1, tile), f32),
            pltpu.VMEM((WAVES, tile, tile), bf16),
            pltpu.VMEM((WAVES, MEMBERS, tile, tile), bf16),
            dma((16,)), dma((MEMBERS,)),
            dma((WAVES, 3)), dma((3,)), dma((WAVES, 3)),
            dma((MEMBERS,)), dma((MEMBERS,)),
            dma((WAVES, MEMBERS)), dma((MEMBERS,)), dma((WAVES, MEMBERS)),
            dma((WAVES, 2, CHUNKS)), dma((WAVES, CHUNKS)),
            dma((WAVES, 2 * MEMBERS, CHUNKS)), dma((WAVES, MEMBERS, CHUNKS)),
        ],
        compiler_params=pltpu.CompilerParams(collective_id=0, has_side_effects=True),
    )(c_matrix, a_upper, b_upper, a_vectors, a_inverse, b_vectors, b_inverse, lam, mu)


def solution(mesh):
    placed = (
        P("row", "col"),
        P("row", "col"),
        P("row", "col"),
        P("row", None),
        P("row", None),
        P("row", None),
        P("row", None),
        P("row"),
        P("row"),
    )
    return jax.shard_map(
        shards, mesh=mesh, in_specs=placed, out_specs=P("row", "col"), check_vma=False
    )
```

```python
import functools

import jax
import jax.numpy as jnp
from jax import lax
from jax.experimental import pallas as pl
from jax.experimental.pallas import tpu as pltpu
from jax.sharding import PartitionSpec as P

WAVES = 3
MEMBERS = 2
CHUNKS = 4
MESH = pl.DeviceIdType.MESH
f32 = jnp.float32
bf16 = jnp.bfloat16


def kernel(
    rows, cols, tile,
    c_hbm, a_hbm, b_hbm, u_hbm, p_hbm, v_hbm, q_hbm, val_hbm,
    out_hbm,
    state, abuf, bbuf, pbuf, ubuf, vbuf, qbuf, vals, xr, xc, part_one, part_three,
    load_sem, out_sem, go_sem,
    vq_send, vq_fsend, vq_recv,
    a_send, a_recv,
    b_send, b_fsend, b_recv,
    xr_send, xr_recv,
    xc_send, xc_recv,
):
    r = lax.axis_index("row")
    c = lax.axis_index("col")
    even_row = r % 2 == 0
    odd_row = r % 2 == 1
    even_col = c % 2 == 0
    mate = r + 1 - 2 * (r % 2)
    other = c + 2 - 4 * ((c // 2) % 2)
    chip_mate = c + 1 - 2 * (c % 2)
    step = tile // CHUNKS
    top = WAVES - 1

    def dot(left, right):
        return jnp.dot(left, right, preferred_element_type=f32)

    def part(ref, member):
        return ref.at[:, pl.ds(member * tile, tile)]

    loads = []

    def load(source, target):
        copy = pltpu.make_async_copy(source, target, load_sem.at[len(loads)])
        copy.start()
        loads.append(copy)
        return copy

    ld_p = load(p_hbm, pbuf)
    ld_c = [load(part(c_hbm, m), state.at[m]) for m in range(MEMBERS)]
    ld_val = load(val_hbm, vals.at[0])
    ld_u = load(u_hbm, ubuf)
    ld_a = [load(part(a_hbm, m), abuf.at[m]) for m in range(MEMBERS)]
    ld_v = load(v_hbm, vbuf.at[0])
    ld_q = load(q_hbm, qbuf.at[0])
    ld_b = [load(part(b_hbm, m), bbuf.at[0, m]) for m in range(MEMBERS)]

    barrier = pltpu.get_barrier_semaphore()
    count = jnp.int32(0)

    def greet(there, to):
        @pl.when(there)
        def _():
            pl.semaphore_signal(barrier, inc=1, device_id=to, device_id_type=MESH)

        return there.astype(jnp.int32)

    for d in (-2, -1, 1, 2):
        count += greet((r + d >= 0) & (r + d < rows), (r + d, c))
        count += greet((c + d >= 0) & (c + d < cols), (r, c + d))
    for d in (-2, 2):
        count += greet((r + d >= 0) & (r + d < rows), (r + d, other))
    pl.semaphore_wait(barrier, count)

    sends = []

    def remote(source, target, send, recv, to):
        return pltpu.make_async_remote_copy(
            src_ref=source, dst_ref=target, send_sem=send, recv_sem=recv,
            device_id=to, device_id_type=MESH,
        )

    def push(condition, *copy, keep=True):
        @pl.when(condition)
        def _():
            remote(*copy).start()

        if keep:
            sends.append((condition, copy))

    def got(target, recv):
        remote(target, target, recv, recv, (r, c)).wait_recv()

    def owns(s):
        j = r - s
        return (j >= 0) & (j // MEMBERS == c)

    home = r // MEMBERS
    away = home + 2 - 4 * ((home // 2) % 2)
    diagonal = c == home
    far = r + 2 < rows
    v_copy = (v_hbm, vbuf.at[2], vq_send.at[2, 0], vq_recv.at[2, 0], (r + 2, c))
    q_copy = (q_hbm, qbuf.at[2], vq_send.at[2, 1], vq_recv.at[2, 1], (r + 2, other))
    helper = c == away
    push(diagonal & far, val_hbm, vals.at[2], vq_send.at[2, 2], vq_recv.at[2, 2], (r + 2, c))
    push(diagonal & far, *v_copy, keep=False)
    push(helper & far, *q_copy, keep=False)
    near = diagonal & even_row & (r + 1 < rows)
    push(near, val_hbm, vals.at[1], vq_send.at[1, 2], vq_recv.at[1, 2], (r + 1, c))
    push(near, v_hbm, vbuf.at[1], vq_send.at[1, 0], vq_recv.at[1, 0], (r + 1, c))
    push(near, q_hbm, qbuf.at[1], vq_send.at[1, 1], vq_recv.at[1, 1], (r + 1, c))

    def push_b(t, m, early):
        l = MEMBERS * c + m
        reach = (l > r) & (r + t < rows)
        reach = reach & ((l <= r + 2) if early else (l > r + 2))
        if t == 1:
            reach = reach & even_row
        source, target = part(b_hbm, m), bbuf.at[t, m]
        push(reach, source, target, b_send.at[t, m], b_recv.at[t, m], (r + t, c))

    for m in range(MEMBERS):
        push_b(2, m, True)
    for m in range(MEMBERS):
        push_b(1, m, True)

    for copy in (ld_p, *ld_c, ld_val):
        copy.wait()
    m_top = jnp.clip(r - top - MEMBERS * c, 0, MEMBERS - 1)

    @pl.when(owns(top))
    def _():
        part_one[...] = dot(pbuf[...], state[m_top].astype(bf16)).astype(bf16)

    def release(condition, copy):
        @pl.when(condition)
        def _():
            remote(*copy).wait_send()
            pl.semaphore_signal(
                go_sem, inc=1, device_id=(r, chip_mate), device_id_type=MESH
            )

    release(diagonal & far, v_copy)
    release(helper & far, q_copy)

    @pl.when(((chip_mate == home) | (chip_mate == away)) & far)
    def _():
        pl.semaphore_wait(go_sem, 1)

    for m in range(MEMBERS):
        push(
            (c > 0) & (r < MEMBERS * c + m),
            part(a_hbm, m), abuf.at[MEMBERS + m], a_send.at[m], a_recv.at[m], (r, c - 1),
        )
    for t in (2, 1):
        for m in range(MEMBERS):
            push_b(t, m, False)

    def update_left(s, m, condition=None):
        i = MEMBERS * c + m + s
        below = (i < rows) & (r < i)
        if condition is not None:
            below = below & condition

        @pl.when(below)
        def _():
            state[m] = state[m] - dot(abuf[m + s], xc[s, m])

    def update_right(s, m, condition=None):
        right = (r - s >= 0) & (MEMBERS * c + m > r - s)
        if condition is not None:
            right = right & condition

        @pl.when(right)
        def _():
            state[m] = state[m] - dot(xr[s], bbuf[s, m])

    def rng(q):
        return pl.ds(q * step, step)

    def is_early(t, m):
        return MEMBERS * c + m <= r - t + 2

    def take_b(t, m, early):
        comes = (r - t >= 0) & (MEMBERS * c + m > r - t)
        comes = comes & (is_early(t, m) if early else jnp.logical_not(is_early(t, m)))

        @pl.when(comes)
        def _():
            got(bbuf.at[t, m], b_recv.at[t, m])

        return comes

    def take_far_b(early):
        for m in range(MEMBERS):
            comes = take_b(2, m, early)
            push(
                comes & odd_row, bbuf.at[2, m], bbuf.at[1, m],
                b_fsend.at[m], b_recv.at[1, m], (r - 1, c),
            )

    def own_member(s):
        return jnp.clip(r - s - MEMBERS * c, 0, MEMBERS - 1)

    def solve(s):
        mine = owns(s)
        m_own = own_member(s)

        @pl.when(mine)
        def _():
            if s < top:
                part_one[...] = dot(pbuf[...], state[m_own].astype(bf16)).astype(bf16)
            if s > 0:
                got(vbuf.at[s], vq_recv.at[s, 0])
                got(vals.at[s], vq_recv.at[s, 2])
            second = dot(part_one[...], vbuf[s])
            wide = jnp.transpose(jnp.broadcast_to(vals[0, 0:1, :], (128, tile)))
            divisor = wide[:, 0:1] + vals[s, 1:2, :]
            part_three[...] = (second / divisor).astype(bf16)
            if s > 0:
                got(qbuf.at[s], vq_recv.at[s, 1])

        half = tile // 2
        for k in range(2):
            @pl.when(mine)
            def _():
                span = pl.ds(k * half, half)
                third = dot(ubuf[span], part_three[...]).astype(bf16)
                solved = dot(third, qbuf[s])
                state[m_own, span] = solved
                xr[s, span] = solved.astype(bf16)

            for q in range(k * CHUNKS // 2, (k + 1) * CHUNKS // 2):
                lane = q % 2
                here = r % 2 == lane
                copy = (xr.at[s, rng(q)], xc.at[s, m_own, rng(q)])
                recv = xc_recv.at[s, m_own, q]
                push(
                    mine & here & (r >= 2),
                    *copy, xc_send.at[s, m_own, q, 0], recv, (r - 2, c),
                )
                push(
                    mine & (odd_row | (jnp.logical_not(here) & (r >= 2))),
                    *copy, xc_send.at[s, m_own, q, 1], recv, (mate, c),
                )
                pass_row(s, q, mine)

    def pass_row(s, q, condition):
        mine = owns(s)
        for d in (1, 2):
            reach = condition & (c + d < cols)
            reach = reach & (even_col if d == 2 else (even_col | mine))
            push(
                reach, xr.at[s, rng(q)], xr.at[s, rng(q)],
                xr_send.at[s, d - 1, q], xr_recv.at[s, q], (r, c + d),
                keep=False,
            )

    def arrivals(s):
        comes_row = (r - s >= 0) & (c > (r - s) // MEMBERS)
        for q in range(CHUNKS):
            @pl.when(comes_row)
            def _():
                got(xr.at[s, rng(q)], xr_recv.at[s, q])

            pass_row(s, q, comes_row)
        for m in range(MEMBERS):
            i = MEMBERS * c + m + s
            pair, source_pair = r // 2, i // 2
            lower = (i < rows) & (pair < source_pair)
            for q in list(range(0, CHUNKS, 1)):
                lane = q % 2
                here = r % 2 == lane
                beside = (i < rows) & (pair == source_pair) & (r != i)
                if lane == 0:
                    beside = beside & (r < i)
                else:
                    beside = beside & ((r < i) | (i >= 2))
                comes = lower | beside
                target = xc.at[s, m, rng(q)]

                @pl.when(comes)
                def _():
                    got(target, xc_recv.at[s, m, q])

                push(
                    comes & here & (r >= 2), target, target,
                    xc_send.at[s, m, q, 0], xc_recv.at[s, m, q], (r - 2, c), keep=False,
                )
                push(
                    lower & here, target, target,
                    xc_send.at[s, m, q, 1], xc_recv.at[s, m, q], (mate, c), keep=False,
                )

    def drain(s):
        mine = owns(s)
        held = (r - s >= 0) & (c >= (r - s) // MEMBERS)
        for q in range(CHUNKS):
            for d in (1, 2):
                reach = held & (c + d < cols)
                reach = reach & (even_col if d == 2 else (even_col | mine))

                @pl.when(reach)
                def _():
                    piece = xr.at[s, rng(q)]
                    remote(
                        piece, piece, xr_send.at[s, d - 1, q], xr_recv.at[s, q], (r, c)
                    ).wait_send()

            lane = q % 2
            here = r % 2 == lane
            for m in range(MEMBERS):
                i = MEMBERS * c + m + s
                pair, source_pair = r // 2, i // 2
                lower = (i < rows) & (pair < source_pair)
                beside = (i < rows) & (pair == source_pair) & (r != i)
                if lane == 0:
                    beside = beside & (r < i)
                else:
                    beside = beside & ((r < i) | (i >= 2))
                piece = xc.at[s, m, rng(q)]

                @pl.when((lower | beside) & here & (r >= 2))
                def _():
                    remote(
                        piece, piece, xc_send.at[s, m, q, 0], xc_recv.at[s, m, q], (r, c)
                    ).wait_send()

                @pl.when(lower & here)
                def _():
                    remote(
                        piece, piece, xc_send.at[s, m, q, 1], xc_recv.at[s, m, q], (r, c)
                    ).wait_send()

    def rest(s, m):
        return jnp.logical_not(owns(s - 1) & (own_member(s - 1) == m))

    ld_u.wait()
    solve(2)
    for k, slot in ((0, vbuf), (2, vals), (1, qbuf)):
        push(
            owns(2) & odd_row, slot.at[2], slot.at[1],
            vq_fsend.at[k], vq_recv.at[1, k], (r - 1, c),
        )
    arrivals(2)
    for copy in ld_a:
        copy.wait()
    for m in range(MEMBERS):
        @pl.when((c + 1 < cols) & (r < MEMBERS * (c + 1) + m))
        def _():
            got(abuf.at[MEMBERS + m], a_recv.at[m])
    take_far_b(True)
    update_left(2, own_member(1), owns(1))
    update_right(2, own_member(1), owns(1))
    solve(1)
    for m in range(MEMBERS):
        update_left(2, m, rest(2, m))
        update_right(2, m, rest(2, m) & is_early(2, m))
    arrivals(1)
    for m in range(MEMBERS):
        take_b(1, m, True)
    for copy in (ld_v, ld_q, *ld_b):
        copy.wait()
    update_left(1, own_member(0), owns(0))
    update_right(1, own_member(0), owns(0))
    solve(0)
    for m in range(MEMBERS):
        update_left(1, m, rest(1, m))
        update_right(1, m, rest(1, m) & is_early(1, m))
    take_far_b(False)
    for m in range(MEMBERS):
        update_right(2, m, jnp.logical_not(is_early(2, m)))
    arrivals(0)
    for m in range(MEMBERS):
        take_b(1, m, False)
    outs = []
    for m in range(MEMBERS):
        update_right(1, m, jnp.logical_not(is_early(1, m)))
        update_left(0, m)
        update_right(0, m)
        copy = pltpu.make_async_copy(state.at[m], part(out_hbm, m), out_sem.at[m])
        copy.start()
        outs.append(copy)
    for condition, copy in sends:
        @pl.when(condition)
        def _():
            remote(*copy).wait_send()
    for s in range(WAVES):
        drain(s)
    for copy in outs:
        copy.wait()


def shards(
    c_matrix, a_upper, b_upper, a_vectors, a_inverse, b_vectors, b_inverse, a_values, b_values
):
    tile = a_vectors.shape[1]
    rows = lax.axis_size("row")
    cols = lax.axis_size("col")
    values = jnp.stack([a_values, b_values]).astype(f32)
    dma = pltpu.SemaphoreType.DMA
    return pl.pallas_call(
        functools.partial(kernel, rows, cols, tile),
        out_shape=jax.ShapeDtypeStruct(c_matrix.shape, f32),
        in_specs=[pl.BlockSpec(memory_space=pl.ANY)] * 8,
        out_specs=pl.BlockSpec(memory_space=pl.ANY),
        scratch_shapes=[
            pltpu.VMEM((MEMBERS, tile, tile), f32),
            pltpu.VMEM((2 * MEMBERS, tile, tile), bf16),
            pltpu.VMEM((WAVES, MEMBERS, tile, tile), bf16),
            pltpu.VMEM((tile, tile), bf16),
            pltpu.VMEM((tile, tile), bf16),
            pltpu.VMEM((WAVES, tile, tile), bf16),
            pltpu.VMEM((WAVES, tile, tile), bf16),
            pltpu.VMEM((WAVES, 2, tile), f32),
            pltpu.VMEM((WAVES, tile, tile), bf16),
            pltpu.VMEM((WAVES, MEMBERS, tile, tile), bf16),
            pltpu.VMEM((tile, tile), bf16),
            pltpu.VMEM((tile, tile), bf16),
            dma((16,)), dma((MEMBERS,)), pltpu.SemaphoreType.REGULAR,
            dma((WAVES, 3)), dma((3,)), dma((WAVES, 3)),
            dma((MEMBERS,)), dma((MEMBERS,)),
            dma((WAVES, MEMBERS)), dma((MEMBERS,)), dma((WAVES, MEMBERS)),
            dma((WAVES, 2, CHUNKS)), dma((WAVES, CHUNKS)),
            dma((WAVES, MEMBERS, CHUNKS, 2)), dma((WAVES, MEMBERS, CHUNKS)),
        ],
        compiler_params=pltpu.CompilerParams(collective_id=0, has_side_effects=True),
    )(c_matrix, a_upper, b_upper, a_vectors, a_inverse, b_vectors, b_inverse, values)


def solution(mesh):
    placed = (
        P("row", "col"),
        P("row", "col"),
        P("row", "col"),
        P("row", None),
        P("row", None),
        P("row", None),
        P("row", None),
        P("row"),
        P("row"),
    )
    return jax.shard_map(
        shards, mesh=mesh, in_specs=placed, out_specs=P("row", "col"), check_vma=False
    )
```

```python
import functools

import jax
import jax.numpy as jnp
from jax import lax
from jax.experimental import pallas as pl
from jax.experimental.pallas import tpu as pltpu
from jax.sharding import PartitionSpec as P

WAVES = 3
MEMBERS = 2
CHUNKS = 4
MESH = pl.DeviceIdType.MESH
f32 = jnp.float32
bf16 = jnp.bfloat16


def kernel(
    rows, cols, tile,
    c_hbm, a_hbm, b_hbm, u_hbm, p_hbm, v_hbm, q_hbm, val_hbm,
    out_hbm,
    state, abuf, bbuf, pbuf, ubuf, vbuf, qbuf, vals, xr, xc, part_one, part_three,
    load_sem, out_sem, go_sem,
    vq_send, vq_fsend, vq_recv,
    a_send, a_recv,
    b_send, b_fsend, b_recv,
    xr_send, xr_recv,
    xc_send, xc_recv,
):
    r = lax.axis_index("row")
    c = lax.axis_index("col")
    even_row = r % 2 == 0
    odd_row = r % 2 == 1
    even_col = c % 2 == 0
    mate = r + 1 - 2 * (r % 2)
    other = c + 2 - 4 * ((c // 2) % 2)
    chip_mate = c + 1 - 2 * (c % 2)
    step = tile // CHUNKS
    top = WAVES - 1

    def dot(left, right):
        return jnp.dot(left, right, preferred_element_type=f32)

    def part(ref, member):
        return ref.at[:, pl.ds(member * tile, tile)]

    loads = []

    def load(source, target):
        copy = pltpu.make_async_copy(source, target, load_sem.at[len(loads)])
        copy.start()
        loads.append(copy)
        return copy

    ld_p = load(p_hbm, pbuf)
    ld_c = [load(part(c_hbm, m), state.at[m]) for m in range(MEMBERS)]
    ld_val = load(val_hbm, vals.at[0])
    ld_u = load(u_hbm, ubuf)
    ld_a = [load(part(a_hbm, m), abuf.at[m]) for m in range(MEMBERS)]
    ld_v = load(v_hbm, vbuf.at[0])
    ld_q = load(q_hbm, qbuf.at[0])
    ld_b = [load(part(b_hbm, m), bbuf.at[0, m]) for m in range(MEMBERS)]

    barrier = pltpu.get_barrier_semaphore()
    count = jnp.int32(0)

    def greet(there, to):
        @pl.when(there)
        def _():
            pl.semaphore_signal(barrier, inc=1, device_id=to, device_id_type=MESH)

        return there.astype(jnp.int32)

    for d in (-2, -1, 1, 2):
        count += greet((r + d >= 0) & (r + d < rows), (r + d, c))
        count += greet((c + d >= 0) & (c + d < cols), (r, c + d))
        count += greet((r + d >= 0) & (r + d < rows), (r + d, other))
    pl.semaphore_wait(barrier, count)

    sends = []

    def remote(source, target, send, recv, to):
        return pltpu.make_async_remote_copy(
            src_ref=source, dst_ref=target, send_sem=send, recv_sem=recv,
            device_id=to, device_id_type=MESH,
        )

    def push(condition, *copy, keep=True):
        @pl.when(condition)
        def _():
            remote(*copy).start()

        if keep:
            sends.append((condition, copy))

    def got(target, recv):
        remote(target, target, recv, recv, (r, c)).wait_recv()

    def owns(s):
        j = r - s
        return (j >= 0) & (j // MEMBERS == c)

    home = r // MEMBERS
    away = home + 2 - 4 * ((home // 2) % 2)
    diagonal = c == home
    far = r + 2 < rows
    v_copy = (v_hbm, vbuf.at[2], vq_send.at[2, 0], vq_recv.at[2, 0], (r + 2, c))
    q_copy = (q_hbm, qbuf.at[2], vq_send.at[2, 1], vq_recv.at[2, 1], (r + 2, other))
    helper = c == away
    push(diagonal & far, val_hbm, vals.at[2], vq_send.at[2, 2], vq_recv.at[2, 2], (r + 2, c))
    push(diagonal & far, *v_copy, keep=False)
    push(helper & far, *q_copy, keep=False)
    push(
        helper & odd_row & (r + 1 < rows),
        q_hbm, qbuf.at[1], vq_send.at[1, 1], vq_recv.at[1, 1], (r + 1, other),
    )
    near = diagonal & even_row & (r + 1 < rows)
    push(near, val_hbm, vals.at[1], vq_send.at[1, 2], vq_recv.at[1, 2], (r + 1, c))
    push(near, v_hbm, vbuf.at[1], vq_send.at[1, 0], vq_recv.at[1, 0], (r + 1, c))
    push(near, q_hbm, qbuf.at[1], vq_send.at[1, 1], vq_recv.at[1, 1], (r + 1, c))

    def push_b(t, m, early):
        l = MEMBERS * c + m
        reach = (l > r) & (r + t < rows)
        reach = reach & ((l <= r + 2) if early else (l > r + 2))
        if t == 1:
            reach = reach & even_row
        source, target = part(b_hbm, m), bbuf.at[t, m]
        push(reach, source, target, b_send.at[t, m], b_recv.at[t, m], (r + t, c))

    for m in range(MEMBERS):
        push_b(2, m, True)
    for m in range(MEMBERS):
        push_b(1, m, True)

    for copy in (ld_p, *ld_c, ld_val):
        copy.wait()
    m_top = jnp.clip(r - top - MEMBERS * c, 0, MEMBERS - 1)

    @pl.when(owns(top))
    def _():
        part_one[...] = dot(pbuf[...], state[m_top].astype(bf16)).astype(bf16)

    def release(condition, copy):
        @pl.when(condition)
        def _():
            remote(*copy).wait_send()
            pl.semaphore_signal(
                go_sem, inc=1, device_id=(r, chip_mate), device_id_type=MESH
            )

    release(diagonal & far, v_copy)
    release(helper & far, q_copy)

    @pl.when(((chip_mate == home) | (chip_mate == away)) & far)
    def _():
        pl.semaphore_wait(go_sem, 1)

    for m in range(MEMBERS):
        push(
            (c > 0) & (r < MEMBERS * c + m),
            part(a_hbm, m), abuf.at[MEMBERS + m], a_send.at[m], a_recv.at[m], (r, c - 1),
        )
    for t in (2, 1):
        for m in range(MEMBERS):
            push_b(t, m, False)

    def update_left(s, m, condition=None):
        i = MEMBERS * c + m + s
        below = (i < rows) & (r < i)
        if condition is not None:
            below = below & condition

        @pl.when(below)
        def _():
            state[m] = state[m] - dot(abuf[m + s], xc[s, m])

    def update_right(s, m, condition=None):
        right = (r - s >= 0) & (MEMBERS * c + m > r - s)
        if condition is not None:
            right = right & condition

        @pl.when(right)
        def _():
            state[m] = state[m] - dot(xr[s], bbuf[s, m])

    def rng(q):
        return pl.ds(q * step, step)

    def is_early(t, m):
        return MEMBERS * c + m <= r - t + 2

    def take_b(t, m, early):
        comes = (r - t >= 0) & (MEMBERS * c + m > r - t)
        comes = comes & (is_early(t, m) if early else jnp.logical_not(is_early(t, m)))

        @pl.when(comes)
        def _():
            got(bbuf.at[t, m], b_recv.at[t, m])

        return comes

    comes_far = []

    def take_far_b(early):
        for m in range(MEMBERS):
            comes = take_b(2, m, early)
            comes_far.append((m, comes))

    def hand_b():
        while comes_far:
            m, comes = comes_far.pop(0)
            push(
                comes & odd_row, bbuf.at[2, m], bbuf.at[1, m],
                b_fsend.at[m], b_recv.at[1, m], (r - 1, c),
            )

    def own_member(s):
        return jnp.clip(r - s - MEMBERS * c, 0, MEMBERS - 1)

    def solve(s):
        mine = owns(s)
        m_own = own_member(s)

        @pl.when(mine)
        def _():
            if s < top:
                part_one[...] = dot(pbuf[...], state[m_own].astype(bf16)).astype(bf16)
            if s > 0:
                got(vbuf.at[s], vq_recv.at[s, 0])
                got(vals.at[s], vq_recv.at[s, 2])

        if s == top:
            for k, slot in ((2, vals), (0, vbuf)):
                push(
                    mine & odd_row, slot.at[2], slot.at[1],
                    vq_fsend.at[k], vq_recv.at[1, k], (r - 1, c),
                )

        @pl.when(mine)
        def _():
            second = dot(part_one[...], vbuf[s])
            wide = jnp.transpose(jnp.broadcast_to(vals[0, 0:1, :], (128, tile)))
            divisor = wide[:, 0:1] + vals[s, 1:2, :]
            part_three[...] = (second / divisor).astype(bf16)
            if s > 0:
                got(qbuf.at[s], vq_recv.at[s, 1])

        half = tile // 2
        for k in range(2):
            @pl.when(mine)
            def _():
                span = pl.ds(k * half, half)
                third = dot(ubuf[span], part_three[...]).astype(bf16)
                solved = dot(third, qbuf[s])
                state[m_own, span] = solved
                xr[s, span] = solved.astype(bf16)

            for q in range(k * CHUNKS // 2, (k + 1) * CHUNKS // 2):
                lane = q % 2
                here = r % 2 == lane
                copy = (xr.at[s, rng(q)], xc.at[s, m_own, rng(q)])
                recv = xc_recv.at[s, m_own, q]
                push(
                    mine & here & (r >= 2),
                    *copy, xc_send.at[s, m_own, q, 0], recv, (r - 2, c),
                )
                push(
                    mine & (odd_row | (jnp.logical_not(here) & (r >= 2))),
                    *copy, xc_send.at[s, m_own, q, 1], recv, (mate, c),
                )
                pass_row(s, q, mine)

    def pass_row(s, q, condition):
        mine = owns(s)
        for d in (1, 2):
            reach = condition & (c + d < cols)
            reach = reach & (even_col if d == 2 else (even_col | mine))
            push(
                reach, xr.at[s, rng(q)], xr.at[s, rng(q)],
                xr_send.at[s, d - 1, q], xr_recv.at[s, q], (r, c + d),
                keep=False,
            )

    def arrivals(s):
        comes_row = (r - s >= 0) & (c > (r - s) // MEMBERS)
        for q in range(CHUNKS):
            @pl.when(comes_row)
            def _():
                got(xr.at[s, rng(q)], xr_recv.at[s, q])

            pass_row(s, q, comes_row)
        for q in range(CHUNKS):
            for m in range(MEMBERS):
                lower, beside, here = route(s, m, q)
                target = xc.at[s, m, rng(q)]

                @pl.when((lower | beside) & here)
                def _():
                    got(target, xc_recv.at[s, m, q])

                push(
                    lower & here, target, target,
                    xc_send.at[s, m, q, 1], xc_recv.at[s, m, q], (mate, c), keep=False,
                )
                push(
                    (lower | beside) & here & (r >= 2), target, target,
                    xc_send.at[s, m, q, 0], xc_recv.at[s, m, q], (r - 2, c), keep=False,
                )

    def settle(s):
        for m in range(MEMBERS):
            for q in range(CHUNKS):
                lower, beside, here = route(s, m, q)

                @pl.when((lower | beside) & jnp.logical_not(here))
                def _():
                    got(xc.at[s, m, rng(q)], xc_recv.at[s, m, q])

    def route(s, m, q):
        i = MEMBERS * c + m + s
        pair, source_pair = r // 2, i // 2
        lower = (i < rows) & (pair < source_pair)
        beside = (i < rows) & (pair == source_pair) & (r != i)
        if q % 2 == 0:
            beside = beside & (r < i)
        else:
            beside = beside & ((r < i) | (i >= 2))
        return lower, beside, r % 2 == q % 2

    def drain(s):
        mine = owns(s)
        held = (r - s >= 0) & (c >= (r - s) // MEMBERS)
        for q in range(CHUNKS):
            for d in (1, 2):
                reach = held & (c + d < cols)
                reach = reach & (even_col if d == 2 else (even_col | mine))

                @pl.when(reach)
                def _():
                    piece = xr.at[s, rng(q)]
                    remote(
                        piece, piece, xr_send.at[s, d - 1, q], xr_recv.at[s, q], (r, c)
                    ).wait_send()

            for m in range(MEMBERS):
                lower, beside, here = route(s, m, q)
                piece = xc.at[s, m, rng(q)]

                @pl.when((lower | beside) & here & (r >= 2))
                def _():
                    remote(
                        piece, piece, xc_send.at[s, m, q, 0], xc_recv.at[s, m, q], (r, c)
                    ).wait_send()

                @pl.when(lower & here)
                def _():
                    remote(
                        piece, piece, xc_send.at[s, m, q, 1], xc_recv.at[s, m, q], (r, c)
                    ).wait_send()

    def rest(s, m):
        return jnp.logical_not(owns(s - 1) & (own_member(s - 1) == m))

    ld_u.wait()
    solve(2)
    arrivals(2)
    for copy in ld_a:
        copy.wait()
    for m in range(MEMBERS):
        @pl.when((c + 1 < cols) & (r < MEMBERS * (c + 1) + m))
        def _():
            got(abuf.at[MEMBERS + m], a_recv.at[m])
    take_far_b(True)
    settle(2)
    update_left(2, own_member(1), owns(1))
    update_right(2, own_member(1), owns(1))
    solve(1)
    hand_b()
    take_far_b(False)
    hand_b()
    for m in range(MEMBERS):
        update_left(2, m, rest(2, m))
        update_right(2, m, rest(2, m) & is_early(2, m))
    arrivals(1)
    for m in range(MEMBERS):
        take_b(1, m, True)
    settle(1)
    for copy in (ld_v, ld_q, *ld_b):
        copy.wait()
    update_left(1, own_member(0), owns(0))
    update_right(1, own_member(0), owns(0))
    solve(0)
    for m in range(MEMBERS):
        update_left(1, m, rest(1, m))
        update_right(1, m, rest(1, m) & is_early(1, m))
    for m in range(MEMBERS):
        update_right(2, m, jnp.logical_not(is_early(2, m)))
    arrivals(0)
    for m in range(MEMBERS):
        take_b(1, m, False)
    settle(0)
    outs = []
    for m in range(MEMBERS):
        update_right(1, m, jnp.logical_not(is_early(1, m)))
        update_left(0, m)
        update_right(0, m)
        copy = pltpu.make_async_copy(state.at[m], part(out_hbm, m), out_sem.at[m])
        copy.start()
        outs.append(copy)
    for condition, copy in sends:
        @pl.when(condition)
        def _():
            remote(*copy).wait_send()
    for s in range(WAVES):
        drain(s)
    for copy in outs:
        copy.wait()


def shards(
    c_matrix, a_upper, b_upper, a_vectors, a_inverse, b_vectors, b_inverse, a_values, b_values
):
    tile = a_vectors.shape[1]
    rows = lax.axis_size("row")
    cols = lax.axis_size("col")
    values = jnp.stack([a_values, b_values]).astype(f32)
    dma = pltpu.SemaphoreType.DMA
    return pl.pallas_call(
        functools.partial(kernel, rows, cols, tile),
        out_shape=jax.ShapeDtypeStruct(c_matrix.shape, f32),
        in_specs=[pl.BlockSpec(memory_space=pl.ANY)] * 8,
        out_specs=pl.BlockSpec(memory_space=pl.ANY),
        scratch_shapes=[
            pltpu.VMEM((MEMBERS, tile, tile), f32),
            pltpu.VMEM((2 * MEMBERS, tile, tile), bf16),
            pltpu.VMEM((WAVES, MEMBERS, tile, tile), bf16),
            pltpu.VMEM((tile, tile), bf16),
            pltpu.VMEM((tile, tile), bf16),
            pltpu.VMEM((WAVES, tile, tile), bf16),
            pltpu.VMEM((WAVES, tile, tile), bf16),
            pltpu.VMEM((WAVES, 2, tile), f32),
            pltpu.VMEM((WAVES, tile, tile), bf16),
            pltpu.VMEM((WAVES, MEMBERS, tile, tile), bf16),
            pltpu.VMEM((tile, tile), bf16),
            pltpu.VMEM((tile, tile), bf16),
            dma((16,)), dma((MEMBERS,)), pltpu.SemaphoreType.REGULAR,
            dma((WAVES, 3)), dma((3,)), dma((WAVES, 3)),
            dma((MEMBERS,)), dma((MEMBERS,)),
            dma((WAVES, MEMBERS)), dma((MEMBERS,)), dma((WAVES, MEMBERS)),
            dma((WAVES, 2, CHUNKS)), dma((WAVES, CHUNKS)),
            dma((WAVES, MEMBERS, CHUNKS, 2)), dma((WAVES, MEMBERS, CHUNKS)),
        ],
        compiler_params=pltpu.CompilerParams(collective_id=0, has_side_effects=True),
    )(c_matrix, a_upper, b_upper, a_vectors, a_inverse, b_vectors, b_inverse, values)


def solution(mesh):
    placed = (
        P("row", "col"),
        P("row", "col"),
        P("row", "col"),
        P("row", None),
        P("row", None),
        P("row", None),
        P("row", None),
        P("row"),
        P("row"),
    )
    return jax.shard_map(
        shards, mesh=mesh, in_specs=placed, out_specs=P("row", "col"), check_vma=False
    )
```

```python
import functools

import jax
import jax.numpy as jnp
from jax import lax
from jax.experimental import pallas as pl
from jax.experimental.pallas import tpu as pltpu
from jax.sharding import PartitionSpec as P

WAVES = 3
MEMBERS = 2
CHUNKS = 4
MESH = pl.DeviceIdType.MESH
f32 = jnp.float32
bf16 = jnp.bfloat16


def kernel(
    rows, cols, tile,
    c_hbm, a_hbm, b_hbm, u_hbm, p_hbm, v_hbm, q_hbm, val_hbm,
    out_hbm,
    state, abuf, bbuf, pbuf, ubuf, vbuf, qbuf, vals, xr, xc, part_one, part_three,
    load_sem, out_sem, go_sem,
    vq_send, vq_fsend, vq_recv,
    a_send, a_recv,
    b_send, b_fsend, b_recv,
    xr_send, xr_recv,
    xc_send, xc_recv,
):
    r = lax.axis_index("row")
    c = lax.axis_index("col")
    even_row = r % 2 == 0
    odd_row = r % 2 == 1
    even_col = c % 2 == 0
    mate = r + 1 - 2 * (r % 2)
    other = c + 2 - 4 * ((c // 2) % 2)
    chip_mate = c + 1 - 2 * (c % 2)
    step = tile // CHUNKS
    top = WAVES - 1

    def dot(left, right):
        return jnp.dot(left, right, preferred_element_type=f32)

    def part(ref, member):
        return ref.at[:, pl.ds(member * tile, tile)]

    loads = []

    def load(source, target):
        copy = pltpu.make_async_copy(source, target, load_sem.at[len(loads)])
        copy.start()
        loads.append(copy)
        return copy

    ld_p = load(p_hbm, pbuf)
    ld_c = [load(part(c_hbm, m), state.at[m]) for m in range(MEMBERS)]
    ld_val = load(val_hbm, vals.at[0])
    ld_u = load(u_hbm, ubuf)
    ld_a = [load(part(a_hbm, m), abuf.at[m]) for m in range(MEMBERS)]
    ld_v = load(v_hbm, vbuf.at[0])
    ld_q = load(q_hbm, qbuf.at[0])
    ld_b = [load(part(b_hbm, m), bbuf.at[0, m]) for m in range(MEMBERS)]

    barrier = pltpu.get_barrier_semaphore()
    count = jnp.int32(0)

    def greet(there, to):
        @pl.when(there)
        def _():
            pl.semaphore_signal(barrier, inc=1, device_id=to, device_id_type=MESH)

        return there.astype(jnp.int32)

    for d in (-2, -1, 1, 2):
        count += greet((r + d >= 0) & (r + d < rows), (r + d, c))
        count += greet((c + d >= 0) & (c + d < cols), (r, c + d))
        count += greet((r + d >= 0) & (r + d < rows), (r + d, other))
    pl.semaphore_wait(barrier, count)

    sends = []

    def remote(source, target, send, recv, to):
        return pltpu.make_async_remote_copy(
            src_ref=source, dst_ref=target, send_sem=send, recv_sem=recv,
            device_id=to, device_id_type=MESH,
        )

    def push(condition, *copy, keep=True):
        @pl.when(condition)
        def _():
            remote(*copy).start()

        if keep:
            sends.append((condition, copy))

    def got(target, recv):
        remote(target, target, recv, recv, (r, c)).wait_recv()

    def owns(s):
        j = r - s
        return (j >= 0) & (j // MEMBERS == c)

    home = r // MEMBERS
    away = home + 2 - 4 * ((home // 2) % 2)
    diagonal = c == home
    far = r + 2 < rows
    v_copy = (v_hbm, vbuf.at[2], vq_send.at[2, 0], vq_recv.at[2, 0], (r + 2, c))
    q_copy = (q_hbm, qbuf.at[2], vq_send.at[2, 1], vq_recv.at[2, 1], (r + 2, other))
    helper = c == away
    push(diagonal & far, val_hbm, vals.at[2], vq_send.at[2, 2], vq_recv.at[2, 2], (r + 2, c))
    push(diagonal & far, *v_copy, keep=False)
    push(helper & far, *q_copy, keep=False)
    push(
        helper & odd_row & (r + 1 < rows),
        q_hbm, qbuf.at[1], vq_send.at[1, 1], vq_recv.at[1, 1], (r + 1, other),
    )
    near = diagonal & even_row & (r + 1 < rows)
    push(near, val_hbm, vals.at[1], vq_send.at[1, 2], vq_recv.at[1, 2], (r + 1, c))
    push(near, v_hbm, vbuf.at[1], vq_send.at[1, 0], vq_recv.at[1, 0], (r + 1, c))
    push(near, q_hbm, qbuf.at[1], vq_send.at[1, 1], vq_recv.at[1, 1], (r + 1, c))

    def push_b(t, m, early):
        l = MEMBERS * c + m
        reach = (l > r) & (r + t < rows)
        reach = reach & ((l <= r + 2) if early else (l > r + 2))
        if t == 1:
            reach = reach & even_row
        source, target = part(b_hbm, m), bbuf.at[t, m]
        push(reach, source, target, b_send.at[t, m], b_recv.at[t, m], (r + t, c))

    for copy in (ld_p, *ld_c, ld_val):
        copy.wait()
    m_top = jnp.clip(r - top - MEMBERS * c, 0, MEMBERS - 1)

    @pl.when(owns(top))
    def _():
        part_one[...] = dot(pbuf[...], state[m_top].astype(bf16)).astype(bf16)

    def release(condition, copy):
        @pl.when(condition)
        def _():
            remote(*copy).wait_send()
            pl.semaphore_signal(
                go_sem, inc=1, device_id=(r, chip_mate), device_id_type=MESH
            )

    release(diagonal & far, v_copy)
    release(helper & far, q_copy)

    @pl.when(((chip_mate == home) | (chip_mate == away)) & far)
    def _():
        pl.semaphore_wait(go_sem, 1)

    for m in range(MEMBERS):
        push_b(2, m, True)
    for m in range(MEMBERS):
        push_b(1, m, True)
    for m in range(MEMBERS):
        push(
            (c > 0) & (r < MEMBERS * c + m),
            part(a_hbm, m), abuf.at[MEMBERS + m], a_send.at[m], a_recv.at[m], (r, c - 1),
        )
    for t in (2, 1):
        for m in range(MEMBERS):
            push_b(t, m, False)

    def update_left(s, m, condition=None):
        i = MEMBERS * c + m + s
        below = (i < rows) & (r < i)
        if condition is not None:
            below = below & condition

        @pl.when(below)
        def _():
            state[m] = state[m] - dot(abuf[m + s], xc[s, m])

    def update_right(s, m, condition=None):
        right = (r - s >= 0) & (MEMBERS * c + m > r - s)
        if condition is not None:
            right = right & condition

        @pl.when(right)
        def _():
            state[m] = state[m] - dot(xr[s], bbuf[s, m])

    def rng(q):
        return pl.ds(q * step, step)

    def is_early(t, m):
        return MEMBERS * c + m <= r - t + 2

    def take_b(t, m, early):
        comes = (r - t >= 0) & (MEMBERS * c + m > r - t)
        comes = comes & (is_early(t, m) if early else jnp.logical_not(is_early(t, m)))

        @pl.when(comes)
        def _():
            got(bbuf.at[t, m], b_recv.at[t, m])

        return comes

    comes_far = []

    def take_far_b(early):
        for m in range(MEMBERS):
            comes = take_b(2, m, early)
            comes_far.append((m, comes))

    def hand_b():
        while comes_far:
            m, comes = comes_far.pop(0)
            push(
                comes & odd_row, bbuf.at[2, m], bbuf.at[1, m],
                b_fsend.at[m], b_recv.at[1, m], (r - 1, c),
            )

    def own_member(s):
        return jnp.clip(r - s - MEMBERS * c, 0, MEMBERS - 1)

    def solve(s):
        mine = owns(s)
        m_own = own_member(s)

        @pl.when(mine)
        def _():
            if s < top:
                part_one[...] = dot(pbuf[...], state[m_own].astype(bf16)).astype(bf16)
            if s > 0:
                got(vbuf.at[s], vq_recv.at[s, 0])
                got(vals.at[s], vq_recv.at[s, 2])

        if s == top:
            for k, slot in ((2, vals), (0, vbuf)):
                push(
                    mine & odd_row, slot.at[2], slot.at[1],
                    vq_fsend.at[k], vq_recv.at[1, k], (r - 1, c),
                )

        @pl.when(mine)
        def _():
            second = dot(part_one[...], vbuf[s])
            wide = jnp.transpose(jnp.broadcast_to(vals[0, 0:1, :], (128, tile)))
            divisor = wide[:, 0:1] + vals[s, 1:2, :]
            part_three[...] = (second / divisor).astype(bf16)
            if s > 0:
                got(qbuf.at[s], vq_recv.at[s, 1])

        half = tile // 2
        for k in range(2):
            @pl.when(mine)
            def _():
                span = pl.ds(k * half, half)
                third = dot(ubuf[span], part_three[...]).astype(bf16)
                solved = dot(third, qbuf[s])
                state[m_own, span] = solved
                xr[s, span] = solved.astype(bf16)

            for q in range(k * CHUNKS // 2, (k + 1) * CHUNKS // 2):
                lane = q % 2
                here = r % 2 == lane
                copy = (xr.at[s, rng(q)], xc.at[s, m_own, rng(q)])
                recv = xc_recv.at[s, m_own, q]
                push(
                    mine & here & (r >= 2),
                    *copy, xc_send.at[s, m_own, q, 0], recv, (r - 2, c),
                )
                push(
                    mine & (odd_row | (jnp.logical_not(here) & (r >= 2))),
                    *copy, xc_send.at[s, m_own, q, 1], recv, (mate, c),
                )
                pass_row(s, q, mine)

    def pass_row(s, q, condition):
        mine = owns(s)
        for d in (1, 2):
            reach = condition & (c + d < cols)
            reach = reach & (even_col if d == 2 else (even_col | mine))
            push(
                reach, xr.at[s, rng(q)], xr.at[s, rng(q)],
                xr_send.at[s, d - 1, q], xr_recv.at[s, q], (r, c + d),
                keep=False,
            )

    def arrivals(s):
        comes_row = (r - s >= 0) & (c > (r - s) // MEMBERS)
        for q in range(CHUNKS):
            @pl.when(comes_row)
            def _():
                got(xr.at[s, rng(q)], xr_recv.at[s, q])

            pass_row(s, q, comes_row)
        for q in range(CHUNKS):
            for m in range(MEMBERS):
                lower, beside, here = route(s, m, q)
                target = xc.at[s, m, rng(q)]

                @pl.when((lower | beside) & here)
                def _():
                    got(target, xc_recv.at[s, m, q])

                push(
                    lower & here, target, target,
                    xc_send.at[s, m, q, 1], xc_recv.at[s, m, q], (mate, c), keep=False,
                )
                push(
                    (lower | beside) & here & (r >= 2), target, target,
                    xc_send.at[s, m, q, 0], xc_recv.at[s, m, q], (r - 2, c), keep=False,
                )

    def settle(s):
        for m in range(MEMBERS):
            for q in range(CHUNKS):
                lower, beside, here = route(s, m, q)

                @pl.when((lower | beside) & jnp.logical_not(here))
                def _():
                    got(xc.at[s, m, rng(q)], xc_recv.at[s, m, q])

    def route(s, m, q):
        i = MEMBERS * c + m + s
        pair, source_pair = r // 2, i // 2
        lower = (i < rows) & (pair < source_pair)
        beside = (i < rows) & (pair == source_pair) & (r != i)
        if q % 2 == 0:
            beside = beside & (r < i)
        else:
            beside = beside & ((r < i) | (i >= 2))
        return lower, beside, r % 2 == q % 2

    def drain(s):
        mine = owns(s)
        held = (r - s >= 0) & (c >= (r - s) // MEMBERS)
        for q in range(CHUNKS):
            for d in (1, 2):
                reach = held & (c + d < cols)
                reach = reach & (even_col if d == 2 else (even_col | mine))

                @pl.when(reach)
                def _():
                    piece = xr.at[s, rng(q)]
                    remote(
                        piece, piece, xr_send.at[s, d - 1, q], xr_recv.at[s, q], (r, c)
                    ).wait_send()

            for m in range(MEMBERS):
                lower, beside, here = route(s, m, q)
                piece = xc.at[s, m, rng(q)]

                @pl.when((lower | beside) & here & (r >= 2))
                def _():
                    remote(
                        piece, piece, xc_send.at[s, m, q, 0], xc_recv.at[s, m, q], (r, c)
                    ).wait_send()

                @pl.when(lower & here)
                def _():
                    remote(
                        piece, piece, xc_send.at[s, m, q, 1], xc_recv.at[s, m, q], (r, c)
                    ).wait_send()

    def rest(s, m):
        return jnp.logical_not(owns(s - 1) & (own_member(s - 1) == m))

    ld_u.wait()
    solve(2)
    arrivals(2)
    for copy in ld_a:
        copy.wait()
    for m in range(MEMBERS):
        @pl.when((c + 1 < cols) & (r < MEMBERS * (c + 1) + m))
        def _():
            got(abuf.at[MEMBERS + m], a_recv.at[m])
    take_far_b(True)
    settle(2)
    update_left(2, own_member(1), owns(1))
    update_right(2, own_member(1), owns(1))
    solve(1)
    hand_b()
    take_far_b(False)
    hand_b()
    for m in range(MEMBERS):
        update_left(2, m, rest(2, m))
        update_right(2, m, rest(2, m) & is_early(2, m))
    arrivals(1)
    for m in range(MEMBERS):
        take_b(1, m, True)
    settle(1)
    for copy in (ld_v, ld_q, *ld_b):
        copy.wait()
    update_left(1, own_member(0), owns(0))
    update_right(1, own_member(0), owns(0))
    solve(0)
    for m in range(MEMBERS):
        update_left(1, m, rest(1, m))
        update_right(1, m, rest(1, m) & is_early(1, m))
    for m in range(MEMBERS):
        update_right(2, m, jnp.logical_not(is_early(2, m)))
    arrivals(0)
    for m in range(MEMBERS):
        take_b(1, m, False)
    settle(0)
    outs = []
    for m in range(MEMBERS):
        update_right(1, m, jnp.logical_not(is_early(1, m)))
        update_left(0, m)
        update_right(0, m)
        copy = pltpu.make_async_copy(state.at[m], part(out_hbm, m), out_sem.at[m])
        copy.start()
        outs.append(copy)
    for condition, copy in sends:
        @pl.when(condition)
        def _():
            remote(*copy).wait_send()
    for s in range(WAVES):
        drain(s)
    for copy in outs:
        copy.wait()


def shards(
    c_matrix, a_upper, b_upper, a_vectors, a_inverse, b_vectors, b_inverse, a_values, b_values
):
    tile = a_vectors.shape[1]
    rows = lax.axis_size("row")
    cols = lax.axis_size("col")
    values = jnp.stack([a_values, b_values]).astype(f32)
    dma = pltpu.SemaphoreType.DMA
    return pl.pallas_call(
        functools.partial(kernel, rows, cols, tile),
        out_shape=jax.ShapeDtypeStruct(c_matrix.shape, f32),
        in_specs=[pl.BlockSpec(memory_space=pl.ANY)] * 8,
        out_specs=pl.BlockSpec(memory_space=pl.ANY),
        scratch_shapes=[
            pltpu.VMEM((MEMBERS, tile, tile), f32),
            pltpu.VMEM((2 * MEMBERS, tile, tile), bf16),
            pltpu.VMEM((WAVES, MEMBERS, tile, tile), bf16),
            pltpu.VMEM((tile, tile), bf16),
            pltpu.VMEM((tile, tile), bf16),
            pltpu.VMEM((WAVES, tile, tile), bf16),
            pltpu.VMEM((WAVES, tile, tile), bf16),
            pltpu.VMEM((WAVES, 2, tile), f32),
            pltpu.VMEM((WAVES, tile, tile), bf16),
            pltpu.VMEM((WAVES, MEMBERS, tile, tile), bf16),
            pltpu.VMEM((tile, tile), bf16),
            pltpu.VMEM((tile, tile), bf16),
            dma((16,)), dma((MEMBERS,)), pltpu.SemaphoreType.REGULAR,
            dma((WAVES, 3)), dma((3,)), dma((WAVES, 3)),
            dma((MEMBERS,)), dma((MEMBERS,)),
            dma((WAVES, MEMBERS)), dma((MEMBERS,)), dma((WAVES, MEMBERS)),
            dma((WAVES, 2, CHUNKS)), dma((WAVES, CHUNKS)),
            dma((WAVES, MEMBERS, CHUNKS, 2)), dma((WAVES, MEMBERS, CHUNKS)),
        ],
        compiler_params=pltpu.CompilerParams(collective_id=0, has_side_effects=True),
    )(c_matrix, a_upper, b_upper, a_vectors, a_inverse, b_vectors, b_inverse, values)


def solution(mesh):
    placed = (
        P("row", "col"),
        P("row", "col"),
        P("row", "col"),
        P("row", None),
        P("row", None),
        P("row", None),
        P("row", None),
        P("row"),
        P("row"),
    )
    return jax.shard_map(
        shards, mesh=mesh, in_specs=placed, out_specs=P("row", "col"), check_vma=False
    )
```
